512 devices in a mesh: pair: 64 (over z, y_hi, core), rows: 8 (over x, y_lo).
Axes of the slice: x: 4, y: 4 (y_hi: 2, y_lo: 2; y = y_hi * 2 + y_lo), z: 16, core: 2. Of those that a mesh axis runs over, the one named last changes fastest.
Arguments:
- snapshot: float32 [1536, 32768], P('rows', 'pair'), may hold values from -40 to 40
- keep_side: int32 [2, 64], P(None, 'pair'), may hold values 0 or 1
Outputs:
- rotated: float32 [1536, 32768], P('rows', 'pair')
The draws below stay inside these ranges and needn't reach their ends.
All inputs are finite; a program needn't handle non-finite values. No bound on the sum of `keep_side` on one device may be relied on, other than what follows from the above.
Results may differ from the reference program's by a relative error of at most 0.00013.
Values sent between devices are 32-bit elements; how exact they have to be, the bound alone decides.
No kernel may reach another device: no remote copies, remote signals or barrier semaphores. Data moves between devices by JAX's collectives and lax.ppermute only.
A program may use at most 64 MiB of HBM per device.

```python
import jax
import jax.numpy as jnp
from jax import lax

BLK = 256
ROUNDS = 2
ROWS = 1536
COLS = 32768
N_PAIR = 64


def draw_snapshot(key, part):
    keys = jax.random.split(jax.random.fold_in(key, 7), 1)
    values = jax.random.normal(keys[0], (ROWS, COLS), jnp.float32)
    return jnp.clip(values, -6.0, 6.0).astype(jnp.float32)


def place_ends(result, rng, smallest, high):
    spot = [jax.random.randint(jax.random.fold_in(rng, axis), (), 0, length) for axis, length in enumerate(result.shape)]
    longest = result.shape.index(max(result.shape))
    beside = spot[:longest] + [(spot[longest] + 1) % result.shape[longest]] + spot[longest + 1:]
    return result.at[tuple(spot)].set(smallest).at[tuple(beside)].set(high)


def setup_inputs(seed: int = 0) -> dict:
    arg_keys = jax.random.split(jax.random.key(seed), 3)
    snapshot = draw_snapshot(jax.random.fold_in(arg_keys[2], 71), 0)
    keep_side = place_ends((jax.random.randint(arg_keys[1], (ROUNDS, N_PAIR), 0, 2) < 1).astype(jnp.int32), jax.random.fold_in(arg_keys[1], 1), 0, 1)
    return {"snapshot": snapshot, "keep_side": keep_side}


EPS = 1e-06

def polar_map(gram, total_rows):
    high = lax.Precision.HIGHEST
    width = gram.shape[0]
    diag_vals = jnp.diagonal(gram)
    inv_norm = lax.rsqrt(diag_vals / total_rows + EPS)
    corr = gram * inv_norm[:, None] * inv_norm[None, :] / total_rows
    scale = jnp.sqrt(jnp.sum(corr * corr) / width)
    e_mat = corr / scale
    eye = jnp.eye(width, dtype=jnp.float32)
    e_two = jnp.dot(e_mat, e_mat, precision=high)
    b_one = (9.0 * e_mat - 6.0 * e_two + jnp.dot(e_mat, e_two, precision=high)) * 0.25
    t_zero = (3.0 * eye - e_mat) * 0.5
    t_one = (3.0 * eye - b_one) * 0.5
    z_two = jnp.dot(t_zero, t_one, precision=high)
    b_two = jnp.dot(jnp.dot(b_one, t_one, precision=high), t_one, precision=high)
    t_two = (3.0 * eye - b_two) * 0.5
    z_three = jnp.dot(z_two, t_two, precision=high)
    return z_three * (inv_norm / jnp.sqrt(scale))[:, None]

def reference(snapshot, keep_side):
    high = lax.Precision.HIGHEST
    total_rows = snapshot.shape[0]
    pairs = snapshot.reshape(total_rows, N_PAIR, 2 * BLK).transpose(1, 0, 2)

    def one_pair(block):
        gram = jnp.dot(block.T, block, precision=high)
        return jnp.dot(block, polar_map(gram, total_rows), precision=high)
    for turn in range(ROUNDS):
        pairs = lax.map(one_pair, pairs)
        first = pairs[:, :, :BLK]
        second = pairs[:, :, BLK:]
        side = keep_side[turn][:, None, None]
        forward = jnp.where(side == 0, first, second)
        backward = jnp.where(side == 0, second, first)
        pairs = jnp.concatenate([jnp.roll(forward, 1, axis=0), jnp.roll(backward, -1, axis=0)], axis=2)
    return pairs.transpose(1, 0, 2).reshape(total_rows, N_PAIR * 2 * BLK)
```

```python
import jax
import jax.numpy as jnp
from jax import lax
from jax.experimental import pallas as pl
from jax.experimental.pallas import tpu as pltpu
from jax.sharding import PartitionSpec as P

ROUNDS = 2


EPS = 1e-06

ROW_PARTS = 8


def shifted(value, axis, steps):
    count = lax.axis_size(axis)
    pairs = [(source, (source + steps) % count) for source in range(count)]
    return lax.ppermute(value, axis, pairs)


def split(value):
    high = value.astype(jnp.bfloat16)
    return high, (value - high.astype(jnp.float32)).astype(jnp.bfloat16)


def dot(left, right):
    return jnp.dot(left, right, preferred_element_type=jnp.float32)


def dot3(left, right):
    left_high, left_low = left
    right_high, right_low = right
    small = dot(left_high, right_low) + dot(left_low, right_high)
    return dot(left_high, right_high) + small


def gram_kernel(left_ref, right_ref, out_ref):
    left = left_ref[...]
    right = right_ref[...]
    half = left.shape[1]
    mid = half // 2
    whole = split(jnp.concatenate([left, right], axis=1))
    left_t = split(left.T)
    right_t = split(right.T)
    upper = dot3(left_t, whole)
    lower = dot3(right_t, (whole[0][:, half:], whole[1][:, half:]))
    parts = out_ref.shape[0]
    rows = mid // parts
    spots = (
        upper[:mid, :half],
        upper[mid:, mid:half],
        lower[:mid],
        lower[mid:, mid:],
        upper[:mid, half:],
        upper[mid:, half:],
    )
    start = 0
    for spot in spots:
        width = spot.shape[1]
        out_ref[:, :, start : start + width] = spot.reshape(parts, rows, width)
        start += width


def sum_kernel(in_ref, out_ref):
    total = in_ref[0]
    for part in range(1, in_ref.shape[0]):
        total = total + in_ref[part]
    for part in range(out_ref.shape[0]):
        out_ref[part] = total


def unpack(packed):
    mid = packed.shape[0]
    a00, a01, a11, b00, b01, b11, c00, c01, c10, c11 = (
        packed[:, i * mid : (i + 1) * mid] for i in range(10)
    )
    rows = (
        (a00, a01, c00, c01),
        (a01.T, a11, c10, c11),
        (c00.T, c10.T, b00, b01),
        (c01.T, c11.T, b01.T, b11),
    )
    gram = jnp.concatenate([jnp.concatenate(row, axis=1) for row in rows], axis=0)
    return gram, (a00, a11, b00, b11)


def polar_kernel(total_rows, side_ref, packed_ref, left_ref, right_ref, fwd_ref, bwd_ref):
    parts, rows, width = packed_ref.shape
    gram, diag_blocks = unpack(packed_ref[...].reshape(parts * rows, width))
    size = gram.shape[0]
    mid = diag_blocks[0].shape[0]
    small_eye = lax.broadcasted_iota(jnp.int32, (mid, mid), 0) == lax.broadcasted_iota(
        jnp.int32, (mid, mid), 1
    )
    picked = [jnp.where(small_eye, block, 0.0) for block in diag_blocks]
    along = jnp.concatenate([jnp.sum(p, axis=0, keepdims=True) for p in picked], axis=1)
    down = jnp.concatenate([jnp.sum(p, axis=1, keepdims=True) for p in picked], axis=0)
    inv_along = lax.rsqrt(along / total_rows + EPS)
    inv_down = lax.rsqrt(down / total_rows + EPS)
    corr = gram * inv_down * inv_along * (1.0 / total_rows)
    square = jnp.sum(jnp.sum(corr * corr, axis=0, keepdims=True), axis=1, keepdims=True)
    scale = jnp.sqrt(square / size)
    eye = lax.broadcasted_iota(jnp.int32, (size, size), 0) == lax.broadcasted_iota(
        jnp.int32, (size, size), 1
    )
    dev = corr * (1.0 / scale) - jnp.where(eye, 1.0, 0.0)
    dev_s = split(dev)
    dev_two = dot3(dev_s, dev_s)
    factor = 0.0625 * dev_two - 0.3125 * dev + jnp.where(eye, 0.375, 0.0)
    z_dev = dot3(split(dev_two), split(factor)) - 0.5 * dev
    z_s = split(z_dev)
    block = jnp.concatenate([left_ref[...], right_ref[...]], axis=1)
    block = block * (inv_along * lax.rsqrt(scale))
    first = block + dot3(split(block), z_s)
    turned = first + dot3(split(first), dev_s)
    turned = turned + dot3(split(turned), z_s)
    turned = turned + dot3(split(turned), z_s)
    new = 1.5 * first - 0.5 * turned
    half = size // 2
    kept = side_ref[0] == 0
    fwd_ref[...] = jnp.where(kept, new[:, :half], new[:, half:])
    bwd_ref[...] = jnp.where(kept, new[:, half:], new[:, :half])


def vmem(count):
    return [pl.BlockSpec(memory_space=pltpu.VMEM)] * count


def local(snapshot, keep_side):
    parts = lax.axis_size("rows")
    rows, size = snapshot.shape
    total_rows = rows * parts
    half = size // 2
    mid = half // 2
    left, right = snapshot[:, :half], snapshot[:, half:]
    packed_shape = jax.ShapeDtypeStruct((parts, mid // parts, 10 * mid), jnp.float32)
    half_shape = jax.ShapeDtypeStruct((rows, half), jnp.float32)
    for turn in range(ROUNDS):
        partial = pl.pallas_call(
            gram_kernel,
            out_shape=packed_shape,
            in_specs=vmem(2),
            out_specs=vmem(1)[0],
            name="gram",
        )(left, right)
        terms = lax.all_to_all(partial, "rows", 0, 0)
        summed = pl.pallas_call(
            sum_kernel,
            out_shape=packed_shape,
            in_specs=vmem(1),
            out_specs=vmem(1)[0],
            name="sum",
        )(terms)
        gathered = lax.all_to_all(summed, "rows", 0, 0)
        forward, backward = pl.pallas_call(
            lambda *refs: polar_kernel(float(total_rows), *refs),
            out_shape=(half_shape, half_shape),
            in_specs=[pl.BlockSpec(memory_space=pltpu.SMEM)] + vmem(3),
            out_specs=tuple(vmem(2)),
            name="polar",
        )(keep_side[turn], gathered, left, right)
        left = shifted(forward, "pair", 1)
        right = shifted(backward, "pair", -1)
    return jnp.concatenate([left, right], axis=1)


def solution(mesh):
    placed = (P("rows", "pair"), P(None, "pair"))
    return jax.shard_map(
        local, mesh=mesh, in_specs=placed, out_specs=P("rows", "pair"), check_vma=False
    )
```

```python
import functools

import jax
import jax.numpy as jnp
from jax import lax
from jax.experimental import pallas as pl
from jax.experimental.pallas import tpu as pltpu
from jax.sharding import PartitionSpec as P

ROUNDS = 2


EPS = 1e-06

ROW_PARTS = 8


def shifted(value, axis, steps):
    count = lax.axis_size(axis)
    pairs = [(source, (source + steps) % count) for source in range(count)]
    return lax.ppermute(value, axis, pairs)


def split(value):
    high = value.astype(jnp.bfloat16)
    return high, (value - high.astype(jnp.float32)).astype(jnp.bfloat16)


def dot(left, right):
    return jnp.dot(left, right, preferred_element_type=jnp.float32)


def dot3(left, right):
    left_high, left_low = left
    right_high, right_low = right
    small = dot(left_high, right_low) + dot(left_low, right_high)
    return dot(left_high, right_high) + small


def joined(refs):
    return jnp.concatenate([ref[...] for ref in refs], axis=1)


def gram_kernel(*refs):
    *block_refs, out_ref = refs
    block = joined(block_refs)
    half = block.shape[1] // 2
    mid = half // 2
    whole = split(block)
    left_t = split(block[:, :half].T)
    right_t = split(block[:, half:].T)
    upper = dot3(left_t, whole)
    lower = dot3(right_t, (whole[0][:, half:], whole[1][:, half:]))
    parts = out_ref.shape[0]
    rows = mid // parts
    spots = (
        upper[:mid, :half],
        upper[mid:, mid:half],
        lower[:mid],
        lower[mid:, mid:],
        upper[:mid, half:],
        upper[mid:, half:],
    )
    start = 0
    for spot in spots:
        width = spot.shape[1]
        out_ref[:, :, start : start + width] = spot.reshape(parts, rows, width)
        start += width


def sum_kernel(in_ref, out_ref):
    total = in_ref[0]
    for part in range(1, in_ref.shape[0]):
        total = total + in_ref[part]
    for part in range(out_ref.shape[0]):
        out_ref[part] = total


def unpack(packed):
    mid = packed.shape[0]
    a00, a01, a11, b00, b01, b11, c00, c01, c10, c11 = (
        packed[:, i * mid : (i + 1) * mid] for i in range(10)
    )
    rows = (
        (a00, a01, c00, c01),
        (a01.T, a11, c10, c11),
        (c00.T, c10.T, b00, b01),
        (c01.T, c11.T, b01.T, b11),
    )
    gram = jnp.concatenate([jnp.concatenate(row, axis=1) for row in rows], axis=0)
    return gram, (a00, a11, b00, b11)


def polar_kernel(total_rows, turn, side_ref, packed_ref, *refs):
    *block_refs, fwd_ref, bwd_ref = refs
    parts, rows, width = packed_ref.shape
    gram, diag_blocks = unpack(packed_ref[...].reshape(parts * rows, width))
    size = gram.shape[0]
    mid = diag_blocks[0].shape[0]
    small_eye = lax.broadcasted_iota(jnp.int32, (mid, mid), 0) == lax.broadcasted_iota(
        jnp.int32, (mid, mid), 1
    )
    picked = [jnp.where(small_eye, block, 0.0) for block in diag_blocks]
    along = jnp.concatenate([jnp.sum(p, axis=0, keepdims=True) for p in picked], axis=1)
    down = jnp.concatenate([jnp.sum(p, axis=1, keepdims=True) for p in picked], axis=0)
    inv_along = lax.rsqrt(along / total_rows + EPS)
    inv_down = lax.rsqrt(down / total_rows + EPS)
    corr = gram * inv_down * inv_along * (1.0 / total_rows)
    square = jnp.sum(jnp.sum(corr * corr, axis=0, keepdims=True), axis=1, keepdims=True)
    scale = jnp.sqrt(square / size)
    eye = lax.broadcasted_iota(jnp.int32, (size, size), 0) == lax.broadcasted_iota(
        jnp.int32, (size, size), 1
    )
    dev = corr * (1.0 / scale) - jnp.where(eye, 1.0, 0.0)
    dev_s = split(dev)
    dev_two = dot3(dev_s, dev_s)
    factor = 0.0625 * dev_two - 0.3125 * dev + jnp.where(eye, 0.375, 0.0)
    z_dev = dot3(split(dev_two), split(factor)) - 0.5 * dev
    z_s = split(z_dev)
    block = joined(block_refs) * (inv_along * lax.rsqrt(scale))
    first = block + dot3(split(block), z_s)
    turned = first + dot3(split(first), dev_s)
    turned = turned + dot3(split(turned), z_s)
    turned = turned + dot3(split(turned), z_s)
    new = 1.5 * first - 0.5 * turned
    half = size // 2
    kept = side_ref[turn] == 0
    fwd_ref[...] = jnp.where(kept, new[:, :half], new[:, half:])
    bwd_ref[...] = jnp.where(kept, new[:, half:], new[:, :half])


def vmem(count):
    return [pl.BlockSpec(memory_space=pltpu.VMEM)] * count


def room(mib):
    return pltpu.CompilerParams(vmem_limit_bytes=mib * 2**20)


def local(snapshot, keep_side):
    parts = lax.axis_size("rows")
    rows, size = snapshot.shape
    total_rows = rows * parts
    half = size // 2
    mid = half // 2
    blocks = (snapshot,)
    sides = keep_side.reshape(keep_side.shape[0])
    packed_shape = jax.ShapeDtypeStruct((parts, mid // parts, 10 * mid), jnp.float32)
    half_shape = jax.ShapeDtypeStruct((rows, half), jnp.float32)
    for turn in range(ROUNDS):
        partial = pl.pallas_call(
            gram_kernel,
            out_shape=packed_shape,
            in_specs=vmem(len(blocks)),
            out_specs=vmem(1)[0],
            name="gram",
            compiler_params=room(8),
        )(*blocks)
        terms = lax.all_to_all(partial, "rows", 0, 0)
        summed = pl.pallas_call(
            sum_kernel,
            out_shape=packed_shape,
            in_specs=vmem(1),
            out_specs=vmem(1)[0],
            name="sum",
            compiler_params=room(8),
        )(terms)
        gathered = lax.all_to_all(summed, "rows", 0, 0)
        forward, backward = pl.pallas_call(
            functools.partial(polar_kernel, float(total_rows), turn),
            out_shape=(half_shape, half_shape),
            in_specs=[pl.BlockSpec(memory_space=pltpu.SMEM)] + vmem(1 + len(blocks)),
            out_specs=tuple(vmem(2)),
            name="polar",
            compiler_params=room(24),
        )(sides, gathered, *blocks)
        blocks = (shifted(forward, "pair", 1), shifted(backward, "pair", -1))
    return jnp.concatenate(blocks, axis=1)


def solution(mesh):
    placed = (P("rows", "pair"), P(None, "pair"))
    return jax.shard_map(
        local, mesh=mesh, in_specs=placed, out_specs=P("rows", "pair"), check_vma=False
    )
```

```python
import functools

import jax
import jax.numpy as jnp
from jax import lax
from jax.experimental import pallas as pl
from jax.experimental.pallas import tpu as pltpu
from jax.sharding import PartitionSpec as P


ROUNDS = 2


EPS = 1e-06


def swapped_near(value, axis):
    count = lax.axis_size(axis)
    return lax.ppermute(value, axis, [(i, i ^ 1) for i in range(count)])


def swapped_far(value, axis):
    count = lax.axis_size(axis)
    pairs = [(i, (i + (1 if i % 2 else -1)) % count) for i in range(count)]
    return lax.ppermute(value, axis, pairs)


def split(value):
    high = value.astype(jnp.bfloat16)
    return high, (value - high.astype(jnp.float32)).astype(jnp.bfloat16)


def dot(left, right):
    return jnp.dot(left, right, preferred_element_type=jnp.float32)


def dot3(left, right):
    left_high, left_low = left
    right_high, right_low = right
    small = dot(left_high, right_low) + dot(left_low, right_high)
    return dot(left_high, right_high) + small


def joined(refs):
    return jnp.concatenate([ref[...] for ref in refs], axis=1)


def gram_kernel(*refs):
    *block_refs, out_ref = refs
    block = joined(block_refs)
    half = block.shape[1] // 2
    mid = half // 2
    whole = split(block)
    left_t = split(block[:, :half].T)
    right_t = split(block[:, half:].T)
    upper = dot3(left_t, whole)
    lower = dot3(right_t, (whole[0][:, half:], whole[1][:, half:]))
    parts = out_ref.shape[0]
    rows = mid // parts
    spots = (
        upper[:mid, :half],
        upper[mid:, mid:half],
        lower[:mid],
        lower[mid:, mid:],
        upper[:mid, half:],
        upper[mid:, half:],
    )
    start = 0
    for spot in spots:
        width = spot.shape[1]
        out_ref[:, :, start : start + width] = spot.reshape(parts, rows, width)
        start += width


def sum_kernel(in_ref, out_ref):
    total = in_ref[0]
    for part in range(1, in_ref.shape[0]):
        total = total + in_ref[part]
    for part in range(out_ref.shape[0]):
        out_ref[part] = total


def unpack(packed):
    mid = packed.shape[0]
    a00, a01, a11, b00, b01, b11, c00, c01, c10, c11 = (
        packed[:, i * mid : (i + 1) * mid] for i in range(10)
    )
    rows = (
        (a00, a01, c00, c01),
        (a01.T, a11, c10, c11),
        (c00.T, c10.T, b00, b01),
        (c01.T, c11.T, b01.T, b11),
    )
    gram = jnp.concatenate([jnp.concatenate(row, axis=1) for row in rows], axis=0)
    return gram, (a00, a11, b00, b11)


def polar_kernel(total_rows, turn, side_ref, packed_ref, *refs):
    *block_refs, near_ref, far_ref = refs
    parts, rows, width = packed_ref.shape
    gram, diag_blocks = unpack(packed_ref[...].reshape(parts * rows, width))
    size = gram.shape[0]
    mid = diag_blocks[0].shape[0]
    small_eye = lax.broadcasted_iota(jnp.int32, (mid, mid), 0) == lax.broadcasted_iota(
        jnp.int32, (mid, mid), 1
    )
    picked = [jnp.where(small_eye, block, 0.0) for block in diag_blocks]
    along = jnp.concatenate([jnp.sum(p, axis=0, keepdims=True) for p in picked], axis=1)
    down = jnp.concatenate([jnp.sum(p, axis=1, keepdims=True) for p in picked], axis=0)
    inv_along = lax.rsqrt(along / total_rows + EPS)
    inv_down = lax.rsqrt(down / total_rows + EPS)
    corr = gram * inv_down * inv_along * (1.0 / total_rows)
    square = jnp.sum(jnp.sum(corr * corr, axis=0, keepdims=True), axis=1, keepdims=True)
    scale = jnp.sqrt(square / size)
    eye = lax.broadcasted_iota(jnp.int32, (size, size), 0) == lax.broadcasted_iota(
        jnp.int32, (size, size), 1
    )
    dev = corr * (1.0 / scale) - jnp.where(eye, 1.0, 0.0)
    dev_s = split(dev)
    dev_two = dot3(dev_s, dev_s)
    factor = 0.0625 * dev_two - 0.3125 * dev + jnp.where(eye, 0.375, 0.0)
    z_dev = dot3(split(dev_two), split(factor)) - 0.5 * dev
    z_s = split(z_dev)
    block = joined(block_refs) * (inv_along * lax.rsqrt(scale))
    first = block + dot3(split(block), z_s)
    turned = first + dot3(split(first), dev_s)
    turned = turned + dot3(split(turned), z_s)
    turned = turned + dot3(split(turned), z_s)
    new = 1.5 * first - 0.5 * turned
    half = size // 2
    side = side_ref[turn] if turn else side_ref[turn] ^ (lax.axis_index("pair") % 2)
    head = (side == 0) == (turn == 0)
    near_ref[...] = jnp.where(head, new[:, :half], new[:, half:])
    far_ref[...] = jnp.where(head, new[:, half:], new[:, :half])


def vmem(count):
    return [pl.BlockSpec(memory_space=pltpu.VMEM)] * count


def room(mib):
    return pltpu.CompilerParams(vmem_limit_bytes=mib * 2**20)


def local(snapshot, keep_side):
    parts = lax.axis_size("rows")
    rows, size = snapshot.shape
    total_rows = rows * parts
    half = size // 2
    mid = half // 2
    blocks = (snapshot,)
    sides = keep_side.reshape(keep_side.shape[0])
    packed_shape = jax.ShapeDtypeStruct((parts, mid // parts, 10 * mid), jnp.float32)
    half_shape = jax.ShapeDtypeStruct((rows, half), jnp.float32)
    for turn in range(ROUNDS):
        partial = pl.pallas_call(
            gram_kernel,
            out_shape=packed_shape,
            in_specs=vmem(len(blocks)),
            out_specs=vmem(1)[0],
            name="gram",
            compiler_params=room(8),
        )(*blocks)
        terms = lax.all_to_all(partial, "rows", 0, 0)
        summed = pl.pallas_call(
            sum_kernel,
            out_shape=packed_shape,
            in_specs=vmem(1),
            out_specs=vmem(1)[0],
            name="sum",
            compiler_params=room(8),
        )(terms)
        gathered = lax.all_to_all(summed, "rows", 0, 0)
        near, far = pl.pallas_call(
            functools.partial(polar_kernel, float(total_rows), turn),
            out_shape=(half_shape, half_shape),
            in_specs=[pl.BlockSpec(memory_space=pltpu.SMEM)] + vmem(1 + len(blocks)),
            out_specs=tuple(vmem(2)),
            name="polar",
            compiler_params=room(24),
        )(sides, gathered, *blocks)
        far = swapped_far(far, "pair")
        near = swapped_near(near, "pair")
        blocks = (near, far)
    odd = lax.axis_index("pair") % 2 == 1
    return jnp.where(odd, jnp.concatenate((near, far), axis=1), jnp.concatenate((far, near), axis=1))


def solution(mesh):
    placed = (P("rows", "pair"), P(None, "pair"))
    return jax.shard_map(
        local, mesh=mesh, in_specs=placed, out_specs=P("rows", "pair"), check_vma=False
    )
```

```python
import functools

import jax
import jax.numpy as jnp
from jax import lax
from jax.experimental import pallas as pl
from jax.experimental.pallas import tpu as pltpu
from jax.sharding import PartitionSpec as P


ROUNDS = 2


EPS = 1e-06


def swapped_near(value, axis):
    count = lax.axis_size(axis)
    return lax.ppermute(value, axis, [(i, i ^ 1) for i in range(count)])


def swapped_far(value, axis):
    count = lax.axis_size(axis)
    pairs = [(i, (i + (1 if i % 2 else -1)) % count) for i in range(count)]
    return lax.ppermute(value, axis, pairs)


def split(value):
    high = value.astype(jnp.bfloat16)
    return high, (value - high.astype(jnp.float32)).astype(jnp.bfloat16)


def dot(left, right):
    return jnp.dot(left, right, preferred_element_type=jnp.float32)


def dot3(left, right):
    left_high, left_low = left
    right_high, right_low = right
    small = dot(left_high, right_low) + dot(left_low, right_high)
    return dot(left_high, right_high) + small


def joined(refs):
    return jnp.concatenate([ref[...] for ref in refs], axis=1)


def gram_kernel(*refs):
    *block_refs, out_ref = refs
    block = joined(block_refs)
    half = block.shape[1] // 2
    mid = half // 2
    whole = split(block)
    left_t = split(block[:, :half].T)
    right_t = split(block[:, half:].T)
    upper = dot3(left_t, whole)
    lower = dot3(right_t, (whole[0][:, half:], whole[1][:, half:]))
    parts = out_ref.shape[0]
    rows = mid // parts
    spots = (
        upper[:mid, :half],
        upper[mid:, mid:half],
        lower[:mid],
        lower[mid:, mid:],
        upper[:mid, half:],
        upper[mid:, half:],
    )
    start = 0
    for spot in spots:
        width = spot.shape[1]
        out_ref[:, :, start : start + width] = spot.reshape(parts, rows, width)
        start += width


def corner_kernel(near_ref, far_ref, out_ref):
    parts, rows, width = out_ref.shape
    half = width // 2
    count = near_ref.shape[0] - 3 * half // 4
    near_t = split(near_ref[:count].T)
    corner = dot3(near_t, split(far_ref[:count]))
    mid = parts * rows
    out_ref[:, :, :half] = corner[:mid].reshape(parts, rows, half)
    out_ref[:, :, half:] = corner[mid:].reshape(parts, rows, half)


def sum_kernel(*refs):
    *far_refs, in_ref, out_ref = refs
    parts, rows, _ = in_ref.shape
    total = in_ref[0]
    for part in range(1, parts):
        total = total + in_ref[part]
    pieces = [total]
    for far_ref in far_refs:
        half = far_ref.shape[1]
        mid = half // 2
        start = far_ref.shape[0] - 3 * rows // 2
        pieces.append(far_ref[start : start + rows])
        tail = far_ref[start + rows :]
        pieces.append(jnp.concatenate([tail[:, :mid], tail[:, mid:]], axis=0))
    total = jnp.concatenate(pieces, axis=1)
    for part in range(parts):
        out_ref[part] = total


CHUNK = 32


def put(value, store):
    for start in range(0, value.shape[0], CHUNK):
        store(slice(start, start + CHUNK), value[start : start + CHUNK])


MATRICES = 5
PAIRS = 7


def polar_scratch(rows, size):
    return (
        [pltpu.VMEM((size, size), jnp.float32)] * MATRICES
        + [pltpu.VMEM((size, size), jnp.bfloat16)] * (2 * PAIRS)
        + [pltpu.VMEM((4, rows, size), jnp.float32)]
        + [pltpu.VMEM((4, rows, size), jnp.bfloat16)] * 2
        + [pltpu.VMEM((size // 2, size // 2), jnp.float32)]
    )


def polar_kernel(total_rows, turn, side_ref, packed_ref, *refs):
    scratch = len(polar_scratch(8, 8))
    *block_refs, near_ref, far_ref = refs[:-scratch]
    refs = refs[-scratch:]
    dev, two, zed, bee, sqr = refs[:MATRICES]
    pairs = refs[MATRICES : MATRICES + 2 * PAIRS]
    dev_s, two_s, mix_s, zed_s, dub_s, bee_s, sqr_s = zip(pairs[::2], pairs[1::2])
    val, val_h, val_l, far_diag = refs[MATRICES + 2 * PAIRS :]
    opening, closing = turn == 0, turn == ROUNDS - 1
    parts, part_rows, _ = packed_ref.shape
    mid = parts * part_rows
    half = 2 * mid
    size = 2 * half
    count = val.shape[1]
    low, high = slice(0, half), slice(half, size)
    halves = (low, high)
    whole = slice(0, size)

    def at(i):
        return slice(i * mid, (i + 1) * mid)

    places = ((0, 0), (1, 1), (2, 2), (3, 3), (0, 1), (2, 3), (0, 2), (0, 3), (1, 2), (1, 3))
    spots = (0, 2, 3, 5, 1, 4, 6, 7, 8, 9) if opening else (-1, -1, 4, 6, -1, 5, 0, 1, 2, 3)
    eye = lax.broadcasted_iota(jnp.int32, (mid, mid), 0) == lax.broadcasted_iota(
        jnp.int32, (mid, mid), 1
    )
    one = jnp.where(eye, 1.0, 0.0)

    def gram_at(place):
        spot = spots[places.index(place)]
        if spot >= 0:
            return packed_ref[:, :, at(spot)].reshape(mid, mid)
        near = block_refs[0]
        if place[0] == 0:
            return near[count : count + mid, at(place[1])]
        return jnp.concatenate([near[count + mid :, at(0)], near[count + mid :, at(1)]], axis=0)

    along, down = [], []
    for i in range(4):
        total = jnp.sum(jnp.where(eye, gram_at((i, i)), 0.0), axis=0, keepdims=True)
        along.append(lax.rsqrt(total + EPS * total_rows))
        down.append(jnp.broadcast_to(along[i], (mid, mid)).T)
    square = jnp.zeros((8, mid), jnp.float32)
    square_off = jnp.zeros((8, mid), jnp.float32)
    for i, j in places:
        corr = gram_at((i, j)) * down[i] * along[j]
        term = jnp.sum((corr * corr).reshape(mid // 8, 8, mid), axis=0)
        if i == j:
            square = square + term
            corr = corr - one
        else:
            square_off = square_off + term
        for row, column, value in ((i, j, corr),) if i == j else ((i, j, corr), (j, i, corr.T)):
            dev[at(row), at(column)] = value
            dev_s[0][at(row), at(column)], dev_s[1][at(row), at(column)] = split(value)
    square = square + 2.0 * square_off
    square = jnp.sum(jnp.sum(square, axis=0, keepdims=True), axis=1, keepdims=True)
    s = lax.rsqrt(square / size)
    t = s - 1.0
    c_four = 0.0625 * s * s * s * s
    c_three = s * s * s * (0.25 * t - 0.3125)
    c_two = s * s * (0.375 + t * (0.375 * t - 0.9375))
    c_one = s * (t * (0.75 + t * (0.25 * t - 0.9375)) - 0.5)
    c_zero = 1.0 + t * (t * (0.375 + t * (0.0625 * t - 0.3125)) - 0.5)

    def times(row, left, right, column):
        return dot3((left[0][row], left[1][row]), (right[0][:, column], right[1][:, column]))

    def symmetric(left, right, store, mirrored):
        for column, row in ((high, whole), (low, low)):

            def keep(piece, value):
                store(piece, column, value)

            put(times(row, left, right, column), keep)
            if row == whole:
                for ref in mirrored:
                    ref[high, low] = ref[low, high].T

    def put_split(pair, piece, column, value):
        pair[0][piece, column], pair[1][piece, column] = split(value)

    def keep_two(piece, column, value):
        two[piece, column] = value
        put_split(two_s, piece, column, value)
        put_split(mix_s, piece, column, c_four * value + c_three * dev[piece, column])

    def keep_zed(piece, column, value):
        value = value + c_two * two[piece, column] + c_one * dev[piece, column]
        zed[piece, column] = value
        put_split(zed_s, piece, column, value)

    def keep_dub(piece, column, value):
        value = value + (2.0 * c_zero) * zed[piece, column]
        two[piece, column] = s * value + (s * c_zero * c_zero) * dev[piece, column]
        put_split(dub_s, piece, column, s * value)

    def keep_bee(piece, column, value):
        value = value + two[piece, column]
        rows = lax.broadcasted_iota(jnp.int32, value.shape, 0) + piece.start
        columns = lax.broadcasted_iota(jnp.int32, value.shape, 1) + column.start
        value = value + jnp.where(rows == columns, s * c_zero * c_zero - 1.0, 0.0)
        bee[piece, column] = value
        put_split(bee_s, piece, column, value)

    def keep_sqr(piece, column, value):
        sqr[piece, column] = value
        put_split(sqr_s, piece, column, value)

    symmetric(dev_s, dev_s, keep_two, two_s + mix_s)
    symmetric(two_s, mix_s, keep_zed, zed_s)

    def keep_val(step):
        def store(piece, value):
            val[step, piece] = value
            val_h[step, piece], val_l[step, piece] = split(value)

        return store

    block = jnp.concatenate([ref[:count] for ref in block_refs], axis=1)
    put(block * jnp.concatenate(along, axis=1), keep_val(0))
    norm = jnp.sqrt(total_rows * s)
    side = side_ref[turn] if turn else side_ref[turn] ^ (lax.axis_index("pair") % 2)
    head = (side == 0) == opening
    if closing:
        plan = ((zed_s, c_zero), (dev_s, 1.0), (zed_s, c_zero), (zed_s, c_zero))
        mine, other = 1.5 * norm, -0.5 * norm * s
    else:
        plan = ((zed_s, c_zero), (bee_s, 0.0))
        mine, other = norm, -0.5 * norm
    for step, (right, factor) in enumerate(plan):
        if right is bee_s:
            symmetric(zed_s, zed_s, keep_dub, dub_s)
            symmetric(dev_s, dub_s, keep_bee, bee_s)
        new = []
        for column in halves:
            product = times(slice(None), (val_h.at[step], val_l.at[step]), right, column)

            def store(piece, value):
                if right is not bee_s:
                    value = value + factor * val[step, piece, column]
                if step == len(plan) - 1:
                    new.append(mine * val[1, piece, column] + other * value)
                else:
                    val[step + 1, piece, column] = value
                    val_h[step + 1, piece, column], val_l[step + 1, piece, column] = split(value)

            put(product, store)
    steps = len(new) // 2
    for k in range(steps):
        piece = slice(k * CHUNK, (k + 1) * CHUNK)
        near_ref[piece] = jnp.where(head, new[k], new[steps + k])
        far_ref[piece] = jnp.where(head, new[steps + k], new[k])
    if closing:
        return
    symmetric(bee_s, bee_s, keep_sqr, sqr_s)
    grams = []
    for column in halves:
        gram = []

        def keep_gram(piece, value):
            piece_in = slice(piece.start + column.start, piece.stop + column.start)
            value = 0.25 * value - 0.75 * sqr[piece_in, column]
            rows = lax.broadcasted_iota(jnp.int32, value.shape, 0) + piece.start
            columns = lax.broadcasted_iota(jnp.int32, value.shape, 1)
            gram.append(total_rows * (value + jnp.where(rows == columns, 1.0, 0.0)))

        put(times(column, sqr_s, bee_s, column), keep_gram)
        grams.append(gram)
    steps = len(grams[0])
    for k in range(steps):
        start = k * CHUNK
        near = jnp.where(head, grams[0][k], grams[1][k])
        far_diag[start : start + CHUNK] = jnp.where(head, grams[1][k], grams[0][k])
        if start < mid:
            near_ref[count + start : count + start + CHUNK] = near
        else:
            into, column = (start - mid) % (mid // 2), at((start - mid) // (mid // 2))
            into = count + mid + into
            near_ref[into : into + CHUNK, column] = near[:, mid:]
    spot = lax.axis_index("rows") * part_rows
    top = far_diag[pl.ds(pl.multiple_of(spot, 8), part_rows)]
    bottom = far_diag[pl.ds(pl.multiple_of(spot + mid, 8), part_rows)][:, mid:]
    far_ref[count : count + part_rows] = top
    far_ref[count + part_rows :, :mid] = bottom[: part_rows // 2]
    far_ref[count + part_rows :, mid:] = bottom[part_rows // 2 :]


def vmem(count):
    return [pl.BlockSpec(memory_space=pltpu.VMEM)] * count


def room(mib):
    return pltpu.CompilerParams(vmem_limit_bytes=mib * 2**20)


def local(snapshot, keep_side):
    parts = lax.axis_size("rows")
    rows, size = snapshot.shape
    total_rows = rows * parts
    half = size // 2
    mid = half // 2
    blocks = (snapshot,)
    sides = keep_side.reshape(keep_side.shape[0])
    part_rows = mid // parts

    def shape(*sizes):
        return jax.ShapeDtypeStruct(sizes, jnp.float32)

    for turn in range(ROUNDS):
        extra = turn < ROUNDS - 1
        sent = 10 * mid if turn == 0 else 4 * mid
        partial = pl.pallas_call(
            corner_kernel if turn else gram_kernel,
            out_shape=shape(parts, part_rows, sent),
            in_specs=vmem(len(blocks)),
            out_specs=vmem(1)[0],
            name="gram",
            compiler_params=room(8),
        )(*blocks)
        terms = lax.all_to_all(partial, "rows", 0, 0)
        slices = blocks[1:]
        summed = pl.pallas_call(
            sum_kernel,
            out_shape=shape(parts, part_rows, sent + 3 * mid * len(slices)),
            in_specs=vmem(1 + len(slices)),
            out_specs=vmem(1)[0],
            name="sum",
            compiler_params=room(8),
        )(*slices, terms)
        gathered = lax.all_to_all(summed, "rows", 0, 0)
        near_rows = rows + extra * 3 * mid // 2
        far_rows = rows + extra * 3 * part_rows // 2
        near, far = pl.pallas_call(
            functools.partial(polar_kernel, float(total_rows), turn),
            out_shape=(shape(near_rows, half), shape(far_rows, half)),
            in_specs=[pl.BlockSpec(memory_space=pltpu.SMEM)] + vmem(1 + len(blocks)),
            out_specs=tuple(vmem(2)),
            scratch_shapes=polar_scratch(rows, size),
            name="polar",
            compiler_params=room(24),
        )(sides, gathered, *blocks)
        far = swapped_far(far, "pair")
        near = swapped_near(near, "pair")
        blocks = (near, far)
    odd = lax.axis_index("pair") % 2 == 1
    return jnp.where(odd, jnp.concatenate((near, far), axis=1), jnp.concatenate((far, near), axis=1))


def solution(mesh):
    placed = (P("rows", "pair"), P(None, "pair"))
    return jax.shard_map(
        local, mesh=mesh, in_specs=placed, out_specs=P("rows", "pair"), check_vma=False
    )
```

```python
import functools

import jax
import jax.numpy as jnp
from jax import lax
from jax.experimental import pallas as pl
from jax.experimental.pallas import tpu as pltpu
from jax.sharding import PartitionSpec as P


ROUNDS = 2


EPS = 1e-06


def swapped_near(value, axis):
    count = lax.axis_size(axis)
    return lax.ppermute(value, axis, [(i, i ^ 1) for i in range(count)])


def swapped_far(value, axis):
    count = lax.axis_size(axis)
    pairs = [(i, (i + (1 if i % 2 else -1)) % count) for i in range(count)]
    return lax.ppermute(value, axis, pairs)


def split(value):
    high = value.astype(jnp.bfloat16)
    return high, (value - high.astype(jnp.float32)).astype(jnp.bfloat16)


def dot(left, right):
    return jnp.dot(left, right, preferred_element_type=jnp.float32)


def dot3(left, right):
    left_high, left_low = left
    right_high, right_low = right
    small = dot(left_high, right_low) + dot(left_low, right_high)
    return dot(left_high, right_high) + small


def joined(refs):
    return jnp.concatenate([ref[...] for ref in refs], axis=1)


def square_index(size):
    return tuple(lax.broadcasted_iota(jnp.int32, (size, size), axis) for axis in (0, 1))


def gram_kernel(*refs):
    *block_refs, out_ref = refs
    block = joined(block_refs)
    half = block.shape[1] // 2
    mid = half // 2
    whole = split(block)
    left_t = split(block[:, :half].T)
    right_t = split(block[:, half:].T)
    upper = dot3(left_t, whole)
    lower = dot3(right_t, (whole[0][:, half:], whole[1][:, half:]))
    parts = out_ref.shape[0]
    rows = mid // parts
    row, column = square_index(mid)
    ends = upper[mid:, mid:half], lower[mid:, mid:]
    diagonals = jnp.zeros((mid, mid), jnp.float32)
    for i, end in enumerate(ends):
        line = jnp.sum(jnp.where(row == column, end, 0.0), axis=0, keepdims=True)
        diagonals = diagonals + jnp.where(row == i, line, 0.0)
    spots = (
        jnp.where(row <= column, upper[:mid, :mid], ends[0]),
        upper[:mid, mid:half],
        jnp.where(row <= column, lower[:mid, :mid], ends[1]),
        lower[:mid, mid:],
        upper[:mid, half:],
        upper[mid:, half:],
        diagonals,
    )
    start = 0
    for spot in spots:
        width = spot.shape[1]
        out_ref[:, :, start : start + width] = spot.reshape(parts, rows, width)
        start += width


def corner_kernel(near_ref, far_ref, out_ref):
    parts, rows, width = out_ref.shape
    half = width // 2
    count = near_ref.shape[0] - 3 * half // 4
    near_t = split(near_ref[:count].T)
    corner = dot3(near_t, split(far_ref[:count]))
    mid = parts * rows
    out_ref[:, :, :half] = corner[:mid].reshape(parts, rows, half)
    out_ref[:, :, half:] = corner[mid:].reshape(parts, rows, half)


def sum_kernel(*refs):
    *far_refs, in_ref, out_ref = refs
    parts, rows, _ = in_ref.shape
    total = in_ref[0]
    for part in range(1, parts):
        total = total + in_ref[part]
    pieces = [total]
    for far_ref in far_refs:
        half = far_ref.shape[1]
        mid = half // 2
        start = far_ref.shape[0] - 3 * rows // 2
        pieces.append(far_ref[start : start + rows])
        tail = far_ref[start + rows :]
        pieces.append(jnp.concatenate([tail[:, :mid], tail[:, mid:]], axis=0))
    total = jnp.concatenate(pieces, axis=1)
    for part in range(parts):
        out_ref[part] = total


CHUNK = 32


def put(value, store):
    for start in range(0, value.shape[0], CHUNK):
        store(slice(start, start + CHUNK), value[start : start + CHUNK])


def place_kernel(near_ref, far_ref, out_ref, sems):
    half = near_ref.shape[1]
    odd = lax.axis_index("pair") % 2
    copies = [
        pltpu.make_async_copy(
            ref, out_ref.at[:, pl.ds(pl.multiple_of(start * half, half), half)], sems.at[i]
        )
        for i, (ref, start) in enumerate(((near_ref, 1 - odd), (far_ref, odd)))
    ]
    for copy in copies:
        copy.start()
    for copy in copies:
        copy.wait()


MATRICES = 5
PAIRS = 7


def polar_scratch(rows, size):
    return (
        [pltpu.VMEM((size, size), jnp.float32)] * MATRICES
        + [pltpu.VMEM((size, size), jnp.bfloat16)] * (2 * PAIRS)
        + [pltpu.VMEM((4, rows, size), jnp.float32)]
        + [pltpu.VMEM((4, rows, size), jnp.bfloat16)] * 2
        + [pltpu.VMEM((size // 2, size // 2), jnp.float32)]
    )


def polar_kernel(total_rows, turn, side_ref, packed_ref, *refs):
    scratch = len(polar_scratch(8, 8))
    *block_refs, near_ref, far_ref = refs[:-scratch]
    refs = refs[-scratch:]
    dev, two, zed, bee, sqr = refs[:MATRICES]
    pairs = refs[MATRICES : MATRICES + 2 * PAIRS]
    dev_s, two_s, mix_s, zed_s, dub_s, bee_s, sqr_s = zip(pairs[::2], pairs[1::2])
    val, val_h, val_l, far_diag = refs[MATRICES + 2 * PAIRS :]
    opening, closing = turn == 0, turn == ROUNDS - 1
    parts, part_rows, _ = packed_ref.shape
    mid = parts * part_rows
    half = 2 * mid
    size = 2 * half
    count = val.shape[1]
    low, high = slice(0, half), slice(half, size)
    halves = (low, high)
    whole = slice(0, size)

    def at(i):
        return slice(i * mid, (i + 1) * mid)

    places = ((0, 0), (1, 1), (2, 2), (3, 3), (0, 1), (2, 3), (0, 2), (0, 3), (1, 2), (1, 3))
    spots = (0, 0, 2, 2, 1, 3, 4, 5, 6, 7) if opening else (-1, -1, 4, 6, -1, 5, 0, 1, 2, 3)
    row_at, column_at = square_index(mid)
    eye = row_at == column_at
    one = jnp.where(eye, 1.0, 0.0)

    def gram_at(place):
        spot = spots[places.index(place)]
        if spot >= 0:
            found = packed_ref[:, :, at(spot)].reshape(mid, mid)
            if not opening or place[0] != place[1]:
                return found
            if place[0] % 2 == 0:
                return jnp.where(row_at <= column_at, found, found.T)
            line = packed_ref[0, place[0] // 2 : place[0] // 2 + 1, at(8)]
            return jnp.where(eye, line, jnp.where(row_at > column_at, found, found.T))
        near = block_refs[0]
        if place[0] == 0:
            return near[count : count + mid, at(place[1])]
        return jnp.concatenate([near[count + mid :, at(0)], near[count + mid :, at(1)]], axis=0)

    along, down = [], []
    for i in range(4):
        total = jnp.sum(jnp.where(eye, gram_at((i, i)), 0.0), axis=0, keepdims=True)
        along.append(lax.rsqrt(total + EPS * total_rows))
        down.append(jnp.broadcast_to(along[i], (mid, mid)).T)
    square = jnp.zeros((8, mid), jnp.float32)
    square_off = jnp.zeros((8, mid), jnp.float32)
    for i, j in places:
        corr = gram_at((i, j)) * down[i] * along[j]
        term = jnp.sum((corr * corr).reshape(mid // 8, 8, mid), axis=0)
        if i == j:
            square = square + term
            corr = corr - one
        else:
            square_off = square_off + term
        for row, column, value in ((i, j, corr),) if i == j else ((i, j, corr), (j, i, corr.T)):
            dev[at(row), at(column)] = value
            dev_s[0][at(row), at(column)], dev_s[1][at(row), at(column)] = split(value)
    square = square + 2.0 * square_off
    square = jnp.sum(jnp.sum(square, axis=0, keepdims=True), axis=1, keepdims=True)
    s = lax.rsqrt(square / size)
    t = s - 1.0
    c_four = 0.0625 * s * s * s * s
    c_three = s * s * s * (0.25 * t - 0.3125)
    c_two = s * s * (0.375 + t * (0.375 * t - 0.9375))
    c_one = s * (t * (0.75 + t * (0.25 * t - 0.9375)) - 0.5)
    c_zero = 1.0 + t * (t * (0.375 + t * (0.0625 * t - 0.3125)) - 0.5)

    def times(row, left, right, column):
        return dot3((left[0][row], left[1][row]), (right[0][:, column], right[1][:, column]))

    def symmetric(left, right, store, mirrored):
        for column, row in ((high, whole), (low, low)):

            def keep(piece, value):
                store(piece, column, value)

            put(times(row, left, right, column), keep)
            if row == whole:
                for ref in mirrored:
                    ref[high, low] = ref[low, high].T

    def put_split(pair, piece, column, value):
        pair[0][piece, column], pair[1][piece, column] = split(value)

    def keep_two(piece, column, value):
        two[piece, column] = value
        put_split(two_s, piece, column, value)
        put_split(mix_s, piece, column, c_four * value + c_three * dev[piece, column])

    def keep_zed(piece, column, value):
        value = value + c_two * two[piece, column] + c_one * dev[piece, column]
        zed[piece, column] = value
        put_split(zed_s, piece, column, value)

    def keep_dub(piece, column, value):
        value = value + (2.0 * c_zero) * zed[piece, column]
        two[piece, column] = s * value + (s * c_zero * c_zero) * dev[piece, column]
        put_split(dub_s, piece, column, s * value)

    def keep_bee(piece, column, value):
        value = value + two[piece, column]
        rows = lax.broadcasted_iota(jnp.int32, value.shape, 0) + piece.start
        columns = lax.broadcasted_iota(jnp.int32, value.shape, 1) + column.start
        value = value + jnp.where(rows == columns, s * c_zero * c_zero - 1.0, 0.0)
        bee[piece, column] = value
        put_split(bee_s, piece, column, value)

    def keep_sqr(piece, column, value):
        sqr[piece, column] = value
        put_split(sqr_s, piece, column, value)

    symmetric(dev_s, dev_s, keep_two, two_s + mix_s)
    symmetric(two_s, mix_s, keep_zed, zed_s)

    def keep_val(step):
        def store(piece, value):
            val[step, piece] = value
            val_h[step, piece], val_l[step, piece] = split(value)

        return store

    block = jnp.concatenate([ref[:count] for ref in block_refs], axis=1)
    put(block * jnp.concatenate(along, axis=1), keep_val(0))
    norm = jnp.sqrt(total_rows * s)
    side = side_ref[turn] if turn else side_ref[turn] ^ (lax.axis_index("pair") % 2)
    head = (side == 0) == opening
    if closing:
        plan = ((zed_s, c_zero), (dev_s, 1.0), (zed_s, c_zero), (zed_s, c_zero))
        mine, other = 1.5 * norm, -0.5 * norm * s
    else:
        plan = ((zed_s, c_zero), (bee_s, 0.0))
        mine, other = norm, -0.5 * norm
    for step, (right, factor) in enumerate(plan):
        if right is bee_s:
            symmetric(zed_s, zed_s, keep_dub, dub_s)
            symmetric(dev_s, dub_s, keep_bee, bee_s)
        new = []
        for column in halves:
            product = times(slice(None), (val_h.at[step], val_l.at[step]), right, column)

            def store(piece, value):
                if right is not bee_s:
                    value = value + factor * val[step, piece, column]
                if step == len(plan) - 1:
                    new.append(mine * val[1, piece, column] + other * value)
                else:
                    val[step + 1, piece, column] = value
                    val_h[step + 1, piece, column], val_l[step + 1, piece, column] = split(value)

            put(product, store)
    steps = len(new) // 2
    for k in range(steps):
        piece = slice(k * CHUNK, (k + 1) * CHUNK)
        near_ref[piece] = jnp.where(head, new[k], new[steps + k])
        far_ref[piece] = jnp.where(head, new[steps + k], new[k])
    if closing:
        return
    symmetric(bee_s, bee_s, keep_sqr, sqr_s)
    grams = []
    for column in halves:
        gram = []

        def keep_gram(piece, value):
            piece_in = slice(piece.start + column.start, piece.stop + column.start)
            value = 0.25 * value - 0.75 * sqr[piece_in, column]
            rows = lax.broadcasted_iota(jnp.int32, value.shape, 0) + piece.start
            columns = lax.broadcasted_iota(jnp.int32, value.shape, 1)
            gram.append(total_rows * (value + jnp.where(rows == columns, 1.0, 0.0)))

        put(times(column, sqr_s, bee_s, column), keep_gram)
        grams.append(gram)
    steps = len(grams[0])
    for k in range(steps):
        start = k * CHUNK
        near = jnp.where(head, grams[0][k], grams[1][k])
        far_diag[start : start + CHUNK] = jnp.where(head, grams[1][k], grams[0][k])
        if start < mid:
            near_ref[count + start : count + start + CHUNK] = near
        else:
            into, column = (start - mid) % (mid // 2), at((start - mid) // (mid // 2))
            into = count + mid + into
            near_ref[into : into + CHUNK, column] = near[:, mid:]
    spot = lax.axis_index("rows") * part_rows
    top = far_diag[pl.ds(pl.multiple_of(spot, 8), part_rows)]
    bottom = far_diag[pl.ds(pl.multiple_of(spot + mid, 8), part_rows)][:, mid:]
    far_ref[count : count + part_rows] = top
    far_ref[count + part_rows :, :mid] = bottom[: part_rows // 2]
    far_ref[count + part_rows :, mid:] = bottom[part_rows // 2 :]


def vmem(count):
    return [pl.BlockSpec(memory_space=pltpu.VMEM)] * count


def room(mib):
    return pltpu.CompilerParams(vmem_limit_bytes=mib * 2**20)


def local(snapshot, keep_side):
    parts = lax.axis_size("rows")
    rows, size = snapshot.shape
    total_rows = rows * parts
    half = size // 2
    mid = half // 2
    blocks = (snapshot,)
    sides = keep_side.reshape(keep_side.shape[0])
    part_rows = mid // parts

    def shape(*sizes):
        return jax.ShapeDtypeStruct(sizes, jnp.float32)

    for turn in range(ROUNDS):
        extra = turn < ROUNDS - 1
        sent = 9 * mid if turn == 0 else 4 * mid
        partial = pl.pallas_call(
            corner_kernel if turn else gram_kernel,
            out_shape=shape(parts, part_rows, sent),
            in_specs=vmem(len(blocks)),
            out_specs=vmem(1)[0],
            name="gram",
            compiler_params=room(8),
        )(*blocks)
        terms = lax.all_to_all(partial, "rows", 0, 0)
        slices = blocks[1:]
        summed = pl.pallas_call(
            sum_kernel,
            out_shape=shape(parts, part_rows, sent + 3 * mid * len(slices)),
            in_specs=vmem(1 + len(slices)),
            out_specs=vmem(1)[0],
            name="sum",
            compiler_params=room(8),
        )(*slices, terms)
        gathered = lax.all_to_all(summed, "rows", 0, 0)
        near_rows = rows + extra * 3 * mid // 2
        far_rows = rows + extra * 3 * part_rows // 2
        near, far = pl.pallas_call(
            functools.partial(polar_kernel, float(total_rows), turn),
            out_shape=(shape(near_rows, half), shape(far_rows, half)),
            in_specs=[pl.BlockSpec(memory_space=pltpu.SMEM)] + vmem(1 + len(blocks)),
            out_specs=tuple(vmem(2)),
            scratch_shapes=polar_scratch(rows, size),
            name="polar",
            compiler_params=room(24),
        )(sides, gathered, *blocks)
        far = swapped_far(far, "pair")
        near = swapped_near(near, "pair")
        blocks = (near, far)
    return pl.pallas_call(
        place_kernel,
        out_shape=shape(rows, size),
        in_specs=vmem(2),
        out_specs=pl.BlockSpec(memory_space=pltpu.HBM),
        scratch_shapes=[pltpu.SemaphoreType.DMA((2,))],
        name="place",
        compiler_params=room(8),
    )(*blocks)


def solution(mesh):
    placed = (P("rows", "pair"), P(None, "pair"))
    return jax.shard_map(
        local, mesh=mesh, in_specs=placed, out_specs=P("rows", "pair"), check_vma=False
    )
```

```python
import functools

import jax
import jax.numpy as jnp
from jax import lax
from jax.experimental import pallas as pl
from jax.experimental.pallas import tpu as pltpu
from jax.sharding import PartitionSpec as P


ROUNDS = 2


EPS = 1e-06


def swapped_near(value, axis):
    count = lax.axis_size(axis)
    return lax.ppermute(value, axis, [(i, i ^ 1) for i in range(count)])


def swapped_far(value, axis):
    count = lax.axis_size(axis)
    pairs = [(i, (i + (1 if i % 2 else -1)) % count) for i in range(count)]
    return lax.ppermute(value, axis, pairs)


def split(value):
    high = value.astype(jnp.bfloat16)
    return high, (value - high.astype(jnp.float32)).astype(jnp.bfloat16)


def dot(left, right):
    return jnp.dot(left, right, preferred_element_type=jnp.float32)


def dot3(left, right):
    left_high, left_low = left
    right_high, right_low = right
    small = dot(left_high, right_low) + dot(left_low, right_high)
    return dot(left_high, right_high) + small


def joined(refs):
    return jnp.concatenate([ref[...] for ref in refs], axis=1)


def square_index(size):
    return tuple(lax.broadcasted_iota(jnp.int32, (size, size), axis) for axis in (0, 1))


def gram_kernel(*refs):
    *block_refs, out_ref = refs
    block = joined(block_refs)
    half = block.shape[1] // 2
    mid = half // 2
    whole = split(block)
    left_t = split(block[:, :half].T)
    right_t = split(block[:, half:].T)
    upper = dot3(left_t, whole)
    lower = dot3(right_t, (whole[0][:, half:], whole[1][:, half:]))
    parts = out_ref.shape[0]
    rows = mid // parts
    row, column = square_index(mid)
    ends = upper[mid:, mid:half], lower[mid:, mid:]
    diagonals = jnp.zeros((mid, mid), jnp.float32)
    for i, end in enumerate(ends):
        line = jnp.sum(jnp.where(row == column, end, 0.0), axis=0, keepdims=True)
        diagonals = diagonals + jnp.where(row == i, line, 0.0)
    spots = (
        jnp.where(row <= column, upper[:mid, :mid], ends[0]),
        upper[:mid, mid:half],
        jnp.where(row <= column, lower[:mid, :mid], ends[1]),
        lower[:mid, mid:],
        upper[:mid, half:],
        upper[mid:, half:],
        diagonals,
    )
    start = 0
    for spot in spots:
        width = spot.shape[1]
        out_ref[:, :, start : start + width] = spot.reshape(parts, rows, width)
        start += width


def corner_kernel(near_ref, far_ref, out_ref):
    parts, rows, width = out_ref.shape
    half = width // 2
    count = near_ref.shape[0] - 3 * half // 4
    near_t = split(near_ref[:count].T)
    corner = dot3(near_t, split(far_ref[:count]))
    mid = parts * rows
    out_ref[:, :, :half] = corner[:mid].reshape(parts, rows, half)
    out_ref[:, :, half:] = corner[mid:].reshape(parts, rows, half)


def sum_kernel(*refs):
    *far_refs, in_ref, out_ref = refs
    parts, rows, _ = in_ref.shape
    total = in_ref[0]
    for part in range(1, parts):
        total = total + in_ref[part]
    pieces = [total]
    for far_ref in far_refs:
        half = far_ref.shape[1]
        mid = half // 2
        start = far_ref.shape[0] - 3 * rows // 2
        pieces.append(far_ref[start : start + rows])
        tail = far_ref[start + rows :]
        pieces.append(jnp.concatenate([tail[:, :mid], tail[:, mid:]], axis=0))
    total = jnp.concatenate(pieces, axis=1)
    for part in range(parts):
        out_ref[part] = total


CHUNK = 32


def put(value, store):
    for start in range(0, value.shape[0], CHUNK):
        store(slice(start, start + CHUNK), value[start : start + CHUNK])


def place_kernel(near_ref, far_ref, out_ref, sems):
    half = near_ref.shape[1]
    odd = lax.axis_index("pair") % 2
    copies = [
        pltpu.make_async_copy(
            ref, out_ref.at[:, pl.ds(pl.multiple_of(start * half, half), half)], sems.at[i]
        )
        for i, (ref, start) in enumerate(((near_ref, 1 - odd), (far_ref, odd)))
    ]
    for copy in copies:
        copy.start()
    for copy in copies:
        copy.wait()


MATRICES = 4
PAIRS = 9


def polar_scratch(rows, size):
    return (
        [pltpu.VMEM((size, size), jnp.float32)] * MATRICES
        + [pltpu.VMEM((size, size), jnp.bfloat16)] * (2 * PAIRS)
        + [pltpu.VMEM((4, rows, size), jnp.float32)]
        + [pltpu.VMEM((4, rows, size), jnp.bfloat16)] * 2
        + [pltpu.VMEM((size // 2, size // 2), jnp.float32)]
    )


def polar_kernel(total_rows, turn, side_ref, packed_ref, *refs):
    scratch = len(polar_scratch(8, 8))
    *block_refs, near_ref, far_ref = refs[:-scratch]
    refs = refs[-scratch:]
    dev, two, zed, bee = refs[:MATRICES]
    pairs = refs[MATRICES : MATRICES + 2 * PAIRS]
    cor_s, dev_s, two_s, mix_s, zed_s, dub_s, bee_s, map_s, way_s = zip(pairs[::2], pairs[1::2])
    val, val_h, val_l, far_diag = refs[MATRICES + 2 * PAIRS :]
    opening, closing = turn == 0, turn == ROUNDS - 1
    parts, part_rows, _ = packed_ref.shape
    mid = parts * part_rows
    half = 2 * mid
    size = 2 * half
    count = val.shape[1]
    low, high = slice(0, half), slice(half, size)
    halves = (low, high)
    whole = slice(0, size)

    def at(i):
        return slice(i * mid, (i + 1) * mid)

    places = ((0, 0), (1, 1), (2, 2), (3, 3), (0, 1), (2, 3), (0, 2), (0, 3), (1, 2), (1, 3))
    spots = (0, 0, 2, 2, 1, 3, 4, 5, 6, 7) if opening else (-1, -1, 4, 6, -1, 5, 0, 1, 2, 3)
    row_at, column_at = square_index(mid)
    eye = row_at == column_at
    one = jnp.where(eye, 1.0, 0.0)

    def gram_at(place):
        spot = spots[places.index(place)]
        if spot >= 0:
            found = packed_ref[:, :, at(spot)].reshape(mid, mid)
            if not opening or place[0] != place[1]:
                return found
            if place[0] % 2 == 0:
                return jnp.where(row_at <= column_at, found, found.T)
            line = packed_ref[0, place[0] // 2 : place[0] // 2 + 1, at(8)]
            return jnp.where(eye, line, jnp.where(row_at > column_at, found, found.T))
        near = block_refs[0]
        if place[0] == 0:
            return near[count : count + mid, at(place[1])]
        return jnp.concatenate([near[count + mid :, at(0)], near[count + mid :, at(1)]], axis=0)

    guard = EPS * total_rows
    totals = [
        jnp.sum(jnp.where(eye, gram_at((i, i)), 0.0), axis=0, keepdims=True) for i in range(4)
    ]
    share = sum(total / (total + guard) for total in totals)
    share = jnp.sum(share, axis=1, keepdims=True) / size
    along = [lax.rsqrt((total + guard) * share) for total in totals]
    down = [jnp.broadcast_to(line, (mid, mid)).T for line in along]
    square = jnp.zeros((8, mid), jnp.float32)
    square_off = jnp.zeros((8, mid), jnp.float32)
    for i, j in places:
        corr = gram_at((i, j)) * down[i] * along[j]
        term = jnp.sum((corr * corr).reshape(mid // 8, 8, mid), axis=0)
        if i == j:
            square = square + term
            cor_s[0][at(i), at(i)], cor_s[1][at(i), at(i)] = split(corr)
            corr = corr - one
        else:
            square_off = square_off + term
        for row, column, value in ((i, j, corr),) if i == j else ((i, j, corr), (j, i, corr.T)):
            dev[at(row), at(column)] = value
            parted = split(value)
            for k in range(2):
                dev_s[k][at(row), at(column)] = parted[k]
                if i != j and not closing:
                    cor_s[k][at(row), at(column)] = parted[k]
    square = square + 2.0 * square_off
    square = jnp.sum(jnp.sum(square, axis=0, keepdims=True), axis=1, keepdims=True)
    s = lax.rsqrt(square / size)
    t = s - 1.0
    c_four = 0.0625 * s * s * s * s
    c_three = s * s * s * (0.25 * t - 0.3125)
    c_two = s * s * (0.375 + t * (0.375 * t - 0.9375))
    c_one = s * (t * (0.75 + t * (0.25 * t - 0.9375)) - 0.5)
    c_zero = 1.0 + t * (t * (0.375 + t * (0.0625 * t - 0.3125)) - 0.5)

    def times(row, left, right, column):
        return dot3((left[0][row], left[1][row]), (right[0][:, column], right[1][:, column]))

    def symmetric(left, right, store, mirrored):
        for column, row in ((high, whole), (low, low)):

            def keep(piece, value):
                store(piece, column, value)

            put(times(row, left, right, column), keep)
            if row == whole:
                for ref in mirrored:
                    ref[high, low] = ref[low, high].T

    def put_split(pair, piece, column, value):
        pair[0][piece, column], pair[1][piece, column] = split(value)

    def keep_two(piece, column, value):
        two[piece, column] = value
        put_split(two_s, piece, column, value)
        put_split(mix_s, piece, column, c_four * value + c_three * dev[piece, column])

    def keep_zed(piece, column, value):
        value = value + c_two * two[piece, column] + c_one * dev[piece, column]
        zed[piece, column] = value
        put_split(zed_s, piece, column, value)

    def keep_dub(piece, column, value):
        value = value + (2.0 * c_zero) * zed[piece, column]
        two[piece, column] = s * value + (s * c_zero * c_zero) * dev[piece, column]
        put_split(dub_s, piece, column, s * value)

    def on_diagonal(piece, column, shape, value):
        rows = lax.broadcasted_iota(jnp.int32, shape, 0) + piece.start
        columns = lax.broadcasted_iota(jnp.int32, shape, 1) + column.start
        return jnp.where(rows == columns, value, 0.0)

    def keep_bee(piece, column, value):
        shift = on_diagonal(piece, column, value.shape, s * c_zero * c_zero - 1.0)
        value = value + two[piece, column] + shift
        bee[piece, column] = value
        put_split(bee_s, piece, column, value)

    def keep_map(piece, column, value):
        value = zed[piece, column] - 0.5 * (c_zero * bee[piece, column] + value)
        value = value + on_diagonal(piece, column, value.shape, c_zero)
        put_split(map_s, piece, column, value)

    def keep_way(piece, column, value):
        put_split(way_s, piece, column, value)

    symmetric(dev_s, dev_s, keep_two, two_s + mix_s)
    symmetric(two_s, mix_s, keep_zed, zed_s)

    def keep_val(step):
        def store(piece, value):
            val[step, piece] = value
            val_h[step, piece], val_l[step, piece] = split(value)

        return store

    block = jnp.concatenate([ref[:count] for ref in block_refs], axis=1)
    put(block * jnp.concatenate(along, axis=1), keep_val(0))
    norm = jnp.sqrt(total_rows * s)
    side = side_ref[turn] if turn else side_ref[turn] ^ (lax.axis_index("pair") % 2)
    head = (side == 0) == opening
    if closing:
        plan = ((zed_s, c_zero), (dev_s, 1.0), (zed_s, c_zero), (zed_s, c_zero))
        mine, other = 1.5 * norm, -0.5 * norm * s
    else:
        symmetric(zed_s, zed_s, keep_dub, dub_s)
        symmetric(dev_s, dub_s, keep_bee, bee_s)
        symmetric(bee_s, zed_s, keep_map, map_s)
        plan = ((map_s, None),)
    for step, (right, factor) in enumerate(plan):
        new = []
        for column in halves:
            product = times(slice(None), (val_h.at[step], val_l.at[step]), right, column)

            def store(piece, value):
                if factor is None:
                    new.append(norm * value)
                    return
                value = value + factor * val[step, piece, column]
                if step == len(plan) - 1:
                    new.append(mine * val[1, piece, column] + other * value)
                else:
                    val[step + 1, piece, column] = value
                    val_h[step + 1, piece, column], val_l[step + 1, piece, column] = split(value)

            put(product, store)
    steps = len(new) // 2
    for k in range(steps):
        piece = slice(k * CHUNK, (k + 1) * CHUNK)
        near_ref[piece] = jnp.where(head, new[k], new[steps + k])
        far_ref[piece] = jnp.where(head, new[steps + k], new[k])
    if closing:
        return
    symmetric(cor_s, map_s, keep_way, way_s)
    grams = []
    for column in halves:
        gram = []

        def keep_gram(piece, value):
            gram.append((total_rows * s) * value)

        put(times(column, map_s, way_s, column), keep_gram)
        grams.append(gram)
    steps = len(grams[0])
    for k in range(steps):
        start = k * CHUNK
        near = jnp.where(head, grams[0][k], grams[1][k])
        far_diag[start : start + CHUNK] = jnp.where(head, grams[1][k], grams[0][k])
        if start < mid:
            near_ref[count + start : count + start + CHUNK] = near
        else:
            into, column = (start - mid) % (mid // 2), at((start - mid) // (mid // 2))
            into = count + mid + into
            near_ref[into : into + CHUNK, column] = near[:, mid:]
    spot = lax.axis_index("rows") * part_rows
    top = far_diag[pl.ds(pl.multiple_of(spot, 8), part_rows)]
    bottom = far_diag[pl.ds(pl.multiple_of(spot + mid, 8), part_rows)][:, mid:]
    far_ref[count : count + part_rows] = top
    far_ref[count + part_rows :, :mid] = bottom[: part_rows // 2]
    far_ref[count + part_rows :, mid:] = bottom[part_rows // 2 :]


def vmem(count):
    return [pl.BlockSpec(memory_space=pltpu.VMEM)] * count


def room(mib):
    return pltpu.CompilerParams(vmem_limit_bytes=mib * 2**20)


def local(snapshot, keep_side):
    parts = lax.axis_size("rows")
    rows, size = snapshot.shape
    total_rows = rows * parts
    half = size // 2
    mid = half // 2
    blocks = (snapshot,)
    sides = keep_side.reshape(keep_side.shape[0])
    part_rows = mid // parts

    def shape(*sizes):
        return jax.ShapeDtypeStruct(sizes, jnp.float32)

    for turn in range(ROUNDS):
        extra = turn < ROUNDS - 1
        sent = 9 * mid if turn == 0 else 4 * mid
        partial = pl.pallas_call(
            corner_kernel if turn else gram_kernel,
            out_shape=shape(parts, part_rows, sent),
            in_specs=vmem(len(blocks)),
            out_specs=vmem(1)[0],
            name="gram",
            compiler_params=room(8),
        )(*blocks)
        terms = lax.all_to_all(partial, "rows", 0, 0)
        slices = blocks[1:]
        summed = pl.pallas_call(
            sum_kernel,
            out_shape=shape(parts, part_rows, sent + 3 * mid * len(slices)),
            in_specs=vmem(1 + len(slices)),
            out_specs=vmem(1)[0],
            name="sum",
            compiler_params=room(8),
        )(*slices, terms)
        gathered = lax.all_to_all(summed, "rows", 0, 0)
        near_rows = rows + extra * 3 * mid // 2
        far_rows = rows + extra * 3 * part_rows // 2
        near, far = pl.pallas_call(
            functools.partial(polar_kernel, float(total_rows), turn),
            out_shape=(shape(near_rows, half), shape(far_rows, half)),
            in_specs=[pl.BlockSpec(memory_space=pltpu.SMEM)] + vmem(1 + len(blocks)),
            out_specs=tuple(vmem(2)),
            scratch_shapes=polar_scratch(rows, size),
            name="polar",
            compiler_params=room(24),
        )(sides, gathered, *blocks)
        far = swapped_far(far, "pair")
        near = swapped_near(near, "pair")
        blocks = (near, far)
    return pl.pallas_call(
        place_kernel,
        out_shape=shape(rows, size),
        in_specs=vmem(2),
        out_specs=pl.BlockSpec(memory_space=pltpu.HBM),
        scratch_shapes=[pltpu.SemaphoreType.DMA((2,))],
        name="place",
        compiler_params=room(8),
    )(*blocks)


def solution(mesh):
    placed = (P("rows", "pair"), P(None, "pair"))
    return jax.shard_map(
        local, mesh=mesh, in_specs=placed, out_specs=P("rows", "pair"), check_vma=False
    )
```

```python
import functools

import jax
import jax.numpy as jnp
from jax import lax
from jax.experimental import pallas as pl
from jax.experimental.pallas import tpu as pltpu
from jax.sharding import PartitionSpec as P


ROUNDS = 2


EPS = 1e-06


def swapped_near(value, axis):
    count = lax.axis_size(axis)
    return lax.ppermute(value, axis, [(i, i ^ 1) for i in range(count)])


def swapped_far(value, axis):
    count = lax.axis_size(axis)
    pairs = [(i, (i + (1 if i % 2 else -1)) % count) for i in range(count)]
    return lax.ppermute(value, axis, pairs)


def split(value):
    high = value.astype(jnp.bfloat16)
    return high, (value - high.astype(jnp.float32)).astype(jnp.bfloat16)


def dot(left, right):
    return jnp.dot(left, right, preferred_element_type=jnp.float32)


def dot3(left, right):
    left_high, left_low = left
    right_high, right_low = right
    small = dot(left_high, right_low) + dot(left_low, right_high)
    return dot(left_high, right_high) + small


def joined(refs):
    return jnp.concatenate([ref[...] for ref in refs], axis=1)


def square_index(size):
    return tuple(lax.broadcasted_iota(jnp.int32, (size, size), axis) for axis in (0, 1))


def gram_kernel(*refs):
    *block_refs, out_ref = refs
    block = joined(block_refs)
    half = block.shape[1] // 2
    mid = half // 2
    whole = split(block)
    left_t = split(block[:, :half].T)
    right_t = split(block[:, half:].T)
    upper = dot3(left_t, whole)
    lower = dot3(right_t, (whole[0][:, half:], whole[1][:, half:]))
    parts = out_ref.shape[0]
    rows = mid // parts
    row, column = square_index(mid)
    ends = upper[mid:, mid:half], lower[mid:, mid:]
    diagonals = []
    for end in ends:
        line = jnp.sum(jnp.where(row == column, end, 0.0), axis=0, keepdims=True)
        diagonals.append(line)
    spots = (
        jnp.where(row <= column, upper[:mid, :mid], ends[0]),
        upper[:mid, mid:half],
        jnp.where(row <= column, lower[:mid, :mid], ends[1]),
        lower[:mid, mid:],
        upper[:mid, half : half + mid],
        upper[:mid, half + mid :],
        upper[mid:, half : half + mid],
        upper[mid:, half + mid :],
    )
    for i, spot in enumerate(spots):
        out_ref[:, i * rows : (i + 1) * rows] = spot.reshape(parts, rows, mid)
    tail = len(spots) * rows
    out_ref[:, tail:] = jnp.zeros((parts, out_ref.shape[1] - tail, mid), jnp.float32)
    out_ref[0, tail : tail + len(diagonals)] = jnp.concatenate(diagonals, axis=0)


def corner_kernel(near_ref, far_ref, out_ref):
    parts, rows, width = out_ref.shape
    half = width // 2
    count = near_ref.shape[0] - 3 * half // 4
    near_t = split(near_ref[:count].T)
    corner = dot3(near_t, split(far_ref[:count]))
    mid = parts * rows
    out_ref[:, :, :half] = corner[:mid].reshape(parts, rows, half)
    out_ref[:, :, half:] = corner[mid:].reshape(parts, rows, half)


def sum_kernel(*refs):
    *far_refs, in_ref, out_ref = refs
    parts, rows, _ = in_ref.shape
    total = in_ref[0]
    for part in range(1, parts):
        total = total + in_ref[part]
    pieces = [total]
    for far_ref in far_refs:
        half = far_ref.shape[1]
        mid = half // 2
        start = far_ref.shape[0] - 3 * rows // 2
        pieces.append(far_ref[start : start + rows])
        tail = far_ref[start + rows :]
        pieces.append(jnp.concatenate([tail[:, :mid], tail[:, mid:]], axis=0))
    total = jnp.concatenate(pieces, axis=1)
    for part in range(parts):
        out_ref[part] = total


CHUNK = 16


def put(value, store):
    for start in range(0, value.shape[0], CHUNK):
        store(slice(start, start + CHUNK), value[start : start + CHUNK])


def place_kernel(near_ref, far_ref, out_ref, sems):
    half = near_ref.shape[1]
    odd = lax.axis_index("pair") % 2
    copies = [
        pltpu.make_async_copy(
            ref, out_ref.at[:, pl.ds(pl.multiple_of(start * half, half), half)], sems.at[i]
        )
        for i, (ref, start) in enumerate(((near_ref, 1 - odd), (far_ref, odd)))
    ]
    for copy in copies:
        copy.start()
    for copy in copies:
        copy.wait()


MATRICES = 4
PAIRS = 9


def polar_scratch(rows, size):
    return (
        [pltpu.VMEM((size, size), jnp.float32)] * MATRICES
        + [pltpu.VMEM((size, size), jnp.bfloat16)] * (2 * PAIRS)
        + [pltpu.VMEM((4, rows, size), jnp.float32)]
        + [pltpu.VMEM((4, rows, size), jnp.bfloat16)] * 2
        + [pltpu.VMEM((size // 2, size // 2), jnp.float32)]
    )


def polar_kernel(total_rows, turn, side_ref, packed_ref, *refs):
    scratch = len(polar_scratch(8, 8))
    *block_refs, near_ref, far_ref = refs[:-scratch]
    refs = refs[-scratch:]
    dev, two, zed, bee = refs[:MATRICES]
    pairs = refs[MATRICES : MATRICES + 2 * PAIRS]
    cor_s, dev_s, two_s, mix_s, zed_s, dub_s, bee_s, map_s, way_s = zip(pairs[::2], pairs[1::2])
    val, val_h, val_l, far_diag = refs[MATRICES + 2 * PAIRS :]
    opening, closing = turn == 0, turn == ROUNDS - 1
    parts = packed_ref.shape[0]
    mid = val.shape[2] // 4
    part_rows = mid // parts
    half = 2 * mid
    size = 2 * half
    count = val.shape[1]
    low, high = slice(0, half), slice(half, size)
    halves = (low, high)
    whole = slice(0, size)

    def at(i):
        return slice(i * mid, (i + 1) * mid)

    places = ((0, 0), (1, 1), (2, 2), (3, 3), (0, 1), (2, 3), (0, 2), (0, 3), (1, 2), (1, 3))
    spots = (0, 0, 2, 2, 1, 3, 4, 5, 6, 7) if opening else (-1, -1, 4, 6, -1, 5, 0, 1, 2, 3)
    row_at, column_at = square_index(mid)
    eye = row_at == column_at
    one = jnp.where(eye, 1.0, 0.0)

    def gram_at(place):
        spot = spots[places.index(place)]
        if spot >= 0:
            if not opening:
                return packed_ref[:, :, at(spot)].reshape(mid, mid)
            found = packed_ref[:, spot * part_rows : (spot + 1) * part_rows].reshape(mid, mid)
            if place[0] != place[1]:
                return found
            if place[0] % 2 == 0:
                return jnp.where(row_at <= column_at, found, found.T)
            start = 8 * part_rows + place[0] // 2
            line = packed_ref[0, start : start + 1]
            return jnp.where(eye, line, jnp.where(row_at > column_at, found, found.T))
        near = block_refs[0]
        if place[0] == 0:
            return near[count : count + mid, at(place[1])]
        return jnp.concatenate([near[count + mid :, at(0)], near[count + mid :, at(1)]], axis=0)

    guard = EPS * total_rows
    totals = [
        jnp.sum(jnp.where(eye, gram_at((i, i)), 0.0), axis=0, keepdims=True) for i in range(4)
    ]
    share = sum(total / (total + guard) for total in totals)
    share = jnp.sum(share, axis=1, keepdims=True) / size
    along = [lax.rsqrt((total + guard) * share) for total in totals]
    down = [jnp.broadcast_to(line, (mid, mid)).T for line in along]
    square = jnp.zeros((8, mid), jnp.float32)
    square_off = jnp.zeros((8, mid), jnp.float32)
    for i, j in places:
        corr = gram_at((i, j)) * down[i] * along[j]
        term = jnp.sum((corr * corr).reshape(mid // 8, 8, mid), axis=0)
        if i == j:
            square = square + term
            cor_s[0][at(i), at(i)], cor_s[1][at(i), at(i)] = split(corr)
            corr = corr - one
        else:
            square_off = square_off + term
        for row, column, value in ((i, j, corr),) if i == j else ((i, j, corr), (j, i, corr.T)):
            dev[at(row), at(column)] = value
            parted = split(value)
            for k in range(2):
                dev_s[k][at(row), at(column)] = parted[k]
                if i != j and not closing:
                    cor_s[k][at(row), at(column)] = parted[k]
    square = square + 2.0 * square_off
    square = jnp.sum(jnp.sum(square, axis=0, keepdims=True), axis=1, keepdims=True)
    s = lax.rsqrt(square / size)
    t = s - 1.0
    c_four = 0.0625 * s * s * s * s
    c_three = s * s * s * (0.25 * t - 0.3125)
    c_two = s * s * (0.375 + t * (0.375 * t - 0.9375))
    c_one = s * (t * (0.75 + t * (0.25 * t - 0.9375)) - 0.5)
    c_zero = 1.0 + t * (t * (0.375 + t * (0.0625 * t - 0.3125)) - 0.5)

    def times(row, left, right, column):
        return dot3((left[0][row], left[1][row]), (right[0][:, column], right[1][:, column]))

    def symmetric(left, right, store, mirrored):
        for column, row in ((high, whole), (low, low)):

            def keep(piece, value):
                store(piece, column, value)

            put(times(row, left, right, column), keep)
            if row == whole:
                for ref in mirrored:
                    ref[high, low] = ref[low, high].T

    def put_split(pair, piece, column, value):
        pair[0][piece, column], pair[1][piece, column] = split(value)

    def keep_two(piece, column, value):
        two[piece, column] = value
        put_split(two_s, piece, column, value)
        put_split(mix_s, piece, column, c_four * value + c_three * dev[piece, column])

    def keep_zed(piece, column, value):
        value = value + c_two * two[piece, column] + c_one * dev[piece, column]
        zed[piece, column] = value
        put_split(zed_s, piece, column, value)

    def keep_dub(piece, column, value):
        value = value + (2.0 * c_zero) * zed[piece, column]
        two[piece, column] = s * value + (s * c_zero * c_zero) * dev[piece, column]
        put_split(dub_s, piece, column, s * value)

    def on_diagonal(piece, column, shape, value):
        rows = lax.broadcasted_iota(jnp.int32, shape, 0) + piece.start
        columns = lax.broadcasted_iota(jnp.int32, shape, 1) + column.start
        return jnp.where(rows == columns, value, 0.0)

    def keep_bee(piece, column, value):
        shift = on_diagonal(piece, column, value.shape, s * c_zero * c_zero - 1.0)
        value = value + two[piece, column] + shift
        bee[piece, column] = value
        put_split(bee_s, piece, column, value)

    def keep_map(piece, column, value):
        value = zed[piece, column] - 0.5 * (c_zero * bee[piece, column] + value)
        value = value + on_diagonal(piece, column, value.shape, c_zero)
        put_split(map_s, piece, column, value)

    def keep_way(piece, column, value):
        put_split(way_s, piece, column, value)

    symmetric(dev_s, dev_s, keep_two, two_s + mix_s)
    symmetric(two_s, mix_s, keep_zed, zed_s)

    def keep_val(step):
        def store(piece, value):
            val[step, piece] = value
            val_h[step, piece], val_l[step, piece] = split(value)

        return store

    block = jnp.concatenate([ref[:count] for ref in block_refs], axis=1)
    put(block * jnp.concatenate(along, axis=1), keep_val(0))
    norm = jnp.sqrt(total_rows * s)
    side = side_ref[turn] if turn else side_ref[turn] ^ (lax.axis_index("pair") % 2)
    head = (side == 0) == opening
    if closing:
        plan = ((zed_s, c_zero), (dev_s, 1.0), (zed_s, c_zero), (zed_s, c_zero))
        mine, other = 1.5 * norm, -0.5 * norm * s
    else:
        symmetric(zed_s, zed_s, keep_dub, dub_s)
        symmetric(dev_s, dub_s, keep_bee, bee_s)
        symmetric(bee_s, zed_s, keep_map, map_s)
        plan = ((map_s, None),)
    for step, (right, factor) in enumerate(plan):
        new = []
        for column in halves:
            product = times(slice(None), (val_h.at[step], val_l.at[step]), right, column)

            def store(piece, value):
                if factor is None:
                    new.append(norm * value)
                    return
                value = value + factor * val[step, piece, column]
                if step == len(plan) - 1:
                    new.append(mine * val[1, piece, column] + other * value)
                else:
                    val[step + 1, piece, column] = value
                    val_h[step + 1, piece, column], val_l[step + 1, piece, column] = split(value)

            put(product, store)
    steps = len(new) // 2
    for k in range(steps):
        piece = slice(k * CHUNK, (k + 1) * CHUNK)
        near_ref[piece] = jnp.where(head, new[k], new[steps + k])
        far_ref[piece] = jnp.where(head, new[steps + k], new[k])
    if closing:
        return
    symmetric(cor_s, map_s, keep_way, way_s)
    grams = []
    for column in halves:
        gram = []

        def keep_gram(piece, value):
            gram.append((total_rows * s) * value)

        put(times(column, map_s, way_s, column), keep_gram)
        grams.append(gram)
    steps = len(grams[0])
    for k in range(steps):
        start = k * CHUNK
        near = jnp.where(head, grams[0][k], grams[1][k])
        far_diag[start : start + CHUNK] = jnp.where(head, grams[1][k], grams[0][k])
        if start < mid:
            near_ref[count + start : count + start + CHUNK] = near
        else:
            into, column = (start - mid) % (mid // 2), at((start - mid) // (mid // 2))
            into = count + mid + into
            near_ref[into : into + CHUNK, column] = near[:, mid:]
    spot = lax.axis_index("rows") * part_rows
    top = far_diag[pl.ds(pl.multiple_of(spot, 8), part_rows)]
    bottom = far_diag[pl.ds(pl.multiple_of(spot + mid, 8), part_rows)][:, mid:]
    far_ref[count : count + part_rows] = top
    far_ref[count + part_rows :, :mid] = bottom[: part_rows // 2]
    far_ref[count + part_rows :, mid:] = bottom[part_rows // 2 :]


def vmem(count):
    return [pl.BlockSpec(memory_space=pltpu.VMEM)] * count


def room(mib):
    return pltpu.CompilerParams(vmem_limit_bytes=mib * 2**20)


def local(snapshot, keep_side):
    parts = lax.axis_size("rows")
    rows, size = snapshot.shape
    total_rows = rows * parts
    half = size // 2
    mid = half // 2
    blocks = (snapshot,)
    sides = keep_side.reshape(keep_side.shape[0])
    part_rows = mid // parts

    def shape(*sizes):
        return jax.ShapeDtypeStruct(sizes, jnp.float32)

    for turn in range(ROUNDS):
        extra = turn < ROUNDS - 1
        sent = (part_rows, 4 * mid) if turn else (8 * part_rows + 8, mid)
        partial = pl.pallas_call(
            corner_kernel if turn else gram_kernel,
            out_shape=shape(parts, *sent),
            in_specs=vmem(len(blocks)),
            out_specs=vmem(1)[0],
            name="gram",
            compiler_params=room(8),
        )(*blocks)
        terms = lax.all_to_all(partial, "rows", 0, 0)
        slices = blocks[1:]
        summed = pl.pallas_call(
            sum_kernel,
            out_shape=shape(parts, sent[0], sent[1] + 3 * mid * len(slices)),
            in_specs=vmem(1 + len(slices)),
            out_specs=vmem(1)[0],
            name="sum",
            compiler_params=room(8),
        )(*slices, terms)
        gathered = lax.all_to_all(summed, "rows", 0, 0)
        near_rows = rows + extra * 3 * mid // 2
        far_rows = rows + extra * 3 * part_rows // 2
        near, far = pl.pallas_call(
            functools.partial(polar_kernel, float(total_rows), turn),
            out_shape=(shape(near_rows, half), shape(far_rows, half)),
            in_specs=[pl.BlockSpec(memory_space=pltpu.SMEM)] + vmem(1 + len(blocks)),
            out_specs=tuple(vmem(2)),
            scratch_shapes=polar_scratch(rows, size),
            name="polar",
            compiler_params=room(24),
        )(sides, gathered, *blocks)
        far = swapped_far(far, "pair")
        near = swapped_near(near, "pair")
        blocks = (near, far)
    return pl.pallas_call(
        place_kernel,
        out_shape=shape(rows, size),
        in_specs=vmem(2),
        out_specs=pl.BlockSpec(memory_space=pltpu.HBM),
        scratch_shapes=[pltpu.SemaphoreType.DMA((2,))],
        name="place",
        compiler_params=room(8),
    )(*blocks)


def solution(mesh):
    placed = (P("rows", "pair"), P(None, "pair"))
    return jax.shard_map(
        local, mesh=mesh, in_specs=placed, out_specs=P("rows", "pair"), check_vma=False
    )
```
